32 devices in a mesh: groups: 2 (over y), sink: 16 (over z, x, core).
Axes of the slice: x: 2, y: 2, z: 4, core: 2. Of those that a mesh axis runs over, the one named last changes fastest.
Arguments:
- eigvecs: bfloat16 [16, 2, 3, 192, 8192], P('groups', None, None, None, 'sink'), parts along dimension 0
- momentum: int32 [6], P('groups'), parts along dimension 0, may hold values from -5 to 5, as said below
- peram: bfloat16 [32, 2, 768, 768], P(('groups', 'sink')), parts along dimension 0, may hold values from -0.009338379 to 0.009338379
- times: int32 [32, 2], P(('groups', 'sink')), parts along dimension 0, may hold values from 0 to 7, as said below
Outputs:
- blocks: bfloat16 [32, 2, 768, 768], P(('groups', 'sink')), parts along dimension 0
The draws below stay inside these ranges and needn't reach their ends.
There are 2 independent parts, one for each index of `groups`. The reference program is written for one: setup_inputs(seed, part) draws one part's arguments, and reference() takes and returns one part's arrays. A program takes and returns all parts, laid end to end along the dimension named above; each array names one. Nothing has to cross between parts.
Inputs may be any that keep to these rules, and one draw needn't show every extreme that they name: `momentum`: the three components are distinct; one is -5 and one is 5. In each of the two columns every timeslice appears exactly 16 // 8 times.
All inputs are finite; a program needn't handle non-finite values.
Results may differ from the reference program's by a relative error of at most 0.0075.
Values may be sent and summed in bfloat16 or wider, within the bound.
A program may use at most 64 MiB of HBM per device.

```python
import math
import jax
import jax.numpy as jnp
from jax import lax

K = 192
NT = 8
SITES_DEV = 512
SITES = 8192
PAIRS = 16
N_SINK = 16


def draw_eigvecs(key, part):
    shape = (NT, 2, 3, K, SITES)
    base = jax.random.normal(key, shape, jnp.float32)
    count = SITES // SITES_DEV
    device = (jnp.arange(SITES, dtype=jnp.int32) // SITES_DEV).astype(jnp.float32)
    ramp = 0.6 + 0.9 * device / (count - 1)
    return (base * ramp * (3.0 * SITES) ** (-0.25)).astype(jnp.bfloat16)


def draw_momentum(key, part):
    middle = jax.random.randint(jax.random.fold_in(key, 7), (1,), -4, 5, dtype=jnp.int32)
    triple = jnp.concatenate([jnp.array([-5, 5], jnp.int32), middle])
    return jax.random.permutation(jax.random.fold_in(key, 8), triple).astype(jnp.int32)


def draw_times(key, part):
    order = jnp.arange(PAIRS, dtype=jnp.int32) % NT
    first = jax.random.permutation(jax.random.fold_in(key, 1), order)
    second = jax.random.permutation(jax.random.fold_in(key, 2), order)
    return jnp.stack([first, second], axis=1).astype(jnp.int32)


def block_scale(stream_key, shape, pieces, smallest, largest):
    def one(axis_at, blocks):
        steps = jax.random.uniform(jax.random.fold_in(jax.random.fold_in(stream_key, 6), axis_at), (blocks,), jnp.float32, smallest / len(pieces), largest / len(pieces))
        return jnp.repeat(jnp.exp(steps), shape[axis_at] // blocks).reshape((-1,) + (1,) * (len(shape) - axis_at - 1))

    factor_of = one(*pieces[0])
    for cut in pieces[1:]:
        factor_of = factor_of * one(*cut)
    return factor_of


def noise(rng, dims, scale, limit, pieces=(), kind=jnp.bfloat16):
    loudness = block_scale(rng, dims, pieces, -0.22, 0.18) if pieces else 1.0
    result = jax.random.normal(rng, dims, jnp.float32) * scale * loudness
    return jnp.minimum(jnp.maximum(result, -limit), limit).astype(kind)


def setup_inputs(seed: int = 0, part: int = 0) -> dict:
    seeds = jax.random.split(jax.random.key(seed), 5)
    own_keys = jax.random.split(jax.random.fold_in(seeds[4], part), 5)
    return {
        "eigvecs": draw_eigvecs(jax.random.fold_in(jax.random.fold_in(seeds[4], part), 71), part),
        "momentum": draw_momentum(jax.random.fold_in(jax.random.fold_in(seeds[4], part), 71), part),
        "peram": noise(own_keys[2], (PAIRS, 2, 4 * K, 4 * K), (0.3 / K), 0.009338379, ((0, 16),)),
        "times": draw_times(jax.random.fold_in(jax.random.fold_in(seeds[4], part), 71), part),
    }


def angles(momentum):
    site = jnp.arange(SITES_DEV * N_SINK, dtype=jnp.int32)
    first = site // SITES_DEV
    local = site % SITES_DEV
    second = local // 16
    third = local % 16
    extent = SITES_DEV // 16
    frac = jnp.mod(momentum[0] * first, N_SINK).astype(jnp.float32) / N_SINK
    frac = frac + jnp.mod(momentum[1] * second, extent).astype(jnp.float32) / extent
    frac = frac + jnp.mod(momentum[2] * third, 16).astype(jnp.float32) / 16.0
    return (2.0 * math.pi) * frac


def rounded(value):
    return lax.optimization_barrier(value.astype(jnp.bfloat16)).astype(jnp.float32)


def slice_elemental(vectors, cosine, sine):
    vec_re = vectors[0].astype(jnp.float32)
    vec_im = vectors[1].astype(jnp.float32)
    rot_re = rounded(cosine * vec_re + sine * vec_im)
    rot_im = rounded(cosine * vec_im - sine * vec_re)
    real = jnp.einsum("ckx,clx->kl", vec_re, rot_re) + jnp.einsum("ckx,clx->kl", vec_im, rot_im)
    imag = jnp.einsum("ckx,clx->kl", vec_re, rot_im) - jnp.einsum("ckx,clx->kl", vec_im, rot_re)
    return jnp.concatenate([real, imag], axis=-1)


def reference(eigvecs, momentum, peram, times):
    theta = angles(momentum)
    cosine = jnp.cos(theta)
    sine = jnp.sin(theta)
    partial_sums = lax.map(lambda vectors: slice_elemental(vectors, cosine, sine), eigvecs)
    elemental = partial_sums.astype(jnp.bfloat16)
    signs = jnp.array([1.0, 1.0, -1.0, -1.0], jnp.float32)

    def one_pair(item):
        block, pair = item
        sink_el = elemental[pair[0]].astype(jnp.float32)
        src_el = elemental[pair[1]].astype(jnp.float32)
        width = sink_el.shape[0]
        a_re = sink_el[:, :width]
        a_im = sink_el[:, width:]
        t_re = jnp.roll(block[0].astype(jnp.float32).reshape(4, width, 4 * width), 2, axis=0) * signs[:, None, None]
        t_im = jnp.roll(block[1].astype(jnp.float32).reshape(4, width, 4 * width), 2, axis=0) * signs[:, None, None]
        x_re = jnp.einsum("kl,alc->akc", a_re, t_re) - jnp.einsum("kl,alc->akc", a_im, t_im)
        x_im = jnp.einsum("kl,alc->akc", a_re, t_im) + jnp.einsum("kl,alc->akc", a_im, t_re)
        x_re = rounded(x_re.reshape(4 * width, 4 * width))
        x_im = rounded(x_im.reshape(4 * width, 4 * width))
        y_re = jnp.roll(x_re.reshape(4 * width, 4, width), 2, axis=1)
        y_im = jnp.roll(x_im.reshape(4 * width, 4, width), 2, axis=1)
        e_re = src_el[:, :width]
        e_im = src_el[:, width:]
        m_re = jnp.einsum("rbl,nl->rbn", y_re, e_re) + jnp.einsum("rbl,nl->rbn", y_im, e_im)
        m_im = jnp.einsum("rbl,nl->rbn", y_im, e_re) - jnp.einsum("rbl,nl->rbn", y_re, e_im)
        return jnp.stack([m_re.reshape(4 * width, 4 * width), m_im.reshape(4 * width, 4 * width)]).astype(jnp.bfloat16)

    return lax.map(one_pair, (peram, times))
```

```python
import functools
import math

import jax
import jax.numpy as jnp
from jax import lax
from jax.experimental import pallas as pl
from jax.experimental.pallas import tpu as pltpu
from jax.sharding import PartitionSpec as P

MESH = pl.DeviceIdType.MESH
NT_DIMS = (((1,), (1,)), ((), ()))
LAG_CORE = 1
LAG_X = 4
AHEAD = 4


def angles(momentum, sites, devices, device):
    local = jnp.arange(sites, dtype=jnp.int32)
    second = local // 16
    third = local % 16
    extent = sites // 16
    frac = jnp.mod(momentum[0] * device, devices).astype(jnp.float32) / devices
    frac = frac + jnp.mod(momentum[1] * second, extent).astype(jnp.float32) / extent
    frac = frac + jnp.mod(momentum[2] * third, 16).astype(jnp.float32) / 16.0
    return 2.0 * math.pi * frac


def wrap(value, size):
    if size & (size - 1) == 0:
        return value & (size - 1)
    return lax.rem(lax.rem(value, size) + size, size)


def elemental_kernel(devices, mom_hbm, times_hbm, eig, landed, tiles, own1, send1, got1, own2, send2, got2,
                     sendz, gotz, gathered, picked, times_all, mom, times, small_sem,
                     load_sem, c_send, c_recv, x_send, x_recv, z_send, z_recv,
                     a_send, a_recv, p_send, p_recv, t_send, t_recv):
    slices, _, colors, width, sites = eig.shape
    planes = devices // 4
    per = slices // planes
    half, quarter = width // 2, width // 4
    me = lax.axis_index("sink")
    x = lax.rem(lax.div(me, 2), 2)
    z = lax.div(me, 4)
    c = me & 1
    q = 2 * c + x

    def at(zz, xx, cc):
        return {"sink": (zz * 2 + xx) * 2 + cc}

    core_mate = at(z, x, 1 - c)
    x_mate = at(z, 1 - x, c)
    mates = [(1 - x, c), (x, 1 - c), (1 - x, 1 - c)]
    others = [lax.rem(z + k, planes) for k in range(1, planes)]

    upper = lax.div(z, 2)
    order = [3 * (1 - upper), 2 - upper, z + 1 - 2 * lax.rem(z, 2), z]
    steps = [(order[s], j) for j in range(per) for s in range(planes)]
    count = len(steps)

    mom_load = pltpu.make_async_copy(mom_hbm, mom, small_sem.at[0])
    mom_load.start()
    times_load = pltpu.make_async_copy(times_hbm, times, small_sem.at[1])
    times_load.start()
    loads = []
    for i, (zt, j) in enumerate(steps):
        load = pltpu.make_async_copy(eig.at[zt * per + j], tiles.at[i], load_sem.at[i])
        loads.append(load)
        if i < AHEAD:
            load.start()

    barrier = pltpu.get_barrier_semaphore()
    for xx, cc in mates:
        pl.semaphore_signal(barrier, inc=1, device_id=at(z, xx, cc), device_id_type=MESH)
    for zz in others:
        pl.semaphore_signal(barrier, inc=1, device_id=at(zz, x, c), device_id_type=MESH)

    mom_load.wait()
    extent = sites // 16
    local = lax.broadcasted_iota(jnp.int32, (8, sites), 1)
    second = local >> 4
    third = local & 15
    first = wrap(mom[0] * me, devices).astype(jnp.float32) / devices
    frac = first + wrap(mom[1] * second, extent).astype(jnp.float32) / extent
    frac = frac + wrap(mom[2] * third, 16).astype(jnp.float32) / 16.0
    theta = (2.0 * math.pi) * frac
    cosine = jnp.cos(theta)[0:1]
    sine = jnp.sin(theta)[0:1]

    def remote(src, dst, ssem, rsem, dev):
        return pltpu.make_async_remote_copy(src_ref=src, dst_ref=dst, send_sem=ssem, recv_sem=rsem,
                                            device_id=dev, device_id_type=MESH)

    sends = []
    core_copies, x_copies = [], []

    def partial_sum(i):
        rot_re, rot_im, neg_re, vec_re, vec_im = [], [], [], [], []
        for col in range(colors):
            v_re = tiles[i, 0, col]
            v_im = tiles[i, 1, col]
            f_re = v_re.astype(jnp.float32)
            f_im = v_im.astype(jnp.float32)
            r_re = (cosine * f_re + sine * f_im).astype(jnp.bfloat16)
            rot_re.append(r_re)
            neg_re.append(-r_re)
            rot_im.append((cosine * f_im - sine * f_re).astype(jnp.bfloat16))
            vec_re.append(v_re)
            vec_im.append(v_im)
        both = jnp.concatenate(vec_re + vec_im, axis=1)
        for_re = jnp.concatenate(rot_re + rot_im, axis=1)
        for_im = jnp.concatenate(rot_im + neg_re, axis=1)
        real = lax.dot_general(both, for_re, NT_DIMS, preferred_element_type=jnp.float32)
        imag = lax.dot_general(both, for_im, NT_DIMS, preferred_element_type=jnp.float32)
        total = jnp.concatenate([real, imag], axis=1)
        own1[i] = total
        send1[i] = total.astype(jnp.bfloat16)

    def start_core(i):
        rows = pl.ds(pl.multiple_of((1 - c) * half, half), half)
        copy = remote(send1.at[i, rows], got1.at[i], c_send.at[i], c_recv.at[i], core_mate)
        copy.start()
        core_copies.append(copy)
        sends.append(copy)

    def core_stage(i):
        core_copies[i].wait_recv()
        total = own1[i, pl.ds(pl.multiple_of(c * half, half), half)] + got1[i].astype(jnp.float32)
        own2[i] = total
        send2[i] = total.astype(jnp.bfloat16)
        rows = pl.ds(pl.multiple_of((1 - x) * quarter, quarter), quarter)
        copy = remote(send2.at[i, rows], got2.at[i], x_send.at[i], x_recv.at[i], x_mate)
        copy.start()
        x_copies.append(copy)
        sends.append(copy)

    mine = []

    def x_stage(i):
        zt, j = steps[i]
        x_copies[i].wait_recv()
        total = own2[i, pl.ds(pl.multiple_of(x * quarter, quarter), quarter)] + got2[i].astype(jnp.float32)
        if i % planes < planes - 1:
            sendz[i] = total.astype(jnp.bfloat16)
            copy = remote(sendz.at[i], gotz.at[z, j], z_send.at[i], z_recv.at[z, j], at(zt, x, c))
            copy.start()
            sends.append(copy)
        else:
            mine.append(total)

    def finish(j):
        total = mine[j]
        for zz in others:
            remote(sendz.at[0], gotz.at[zz, j], z_send.at[0], z_recv.at[zz, j], at(zz, x, c)).wait_recv()
            total = total + gotz[zz, j].astype(jnp.float32)
        gathered[z * per + j] = total.astype(jnp.bfloat16)
        block = gathered.at[z * per + j]
        for k in reversed(range(len(others))):
            zz = others[k]
            copy = remote(block, block, a_send.at[k, j], a_recv.at[z, j], at(zz, x, c))
            copy.start()
            sends.append(copy)

    last = count - 1

    def after(i):
        start_core(i)
        if i >= LAG_CORE:
            core_stage(i - LAG_CORE)
        if i >= LAG_X:
            x_stage(i - LAG_X)

    for i in range(count):
        loads[i].wait()
        if i + AHEAD < count:
            loads[i + AHEAD].start()
        partial_sum(i)
        if i == 0:
            pl.semaphore_wait(barrier, len(mates) + len(others))
            times_load.wait()
            for m, (xx, cc) in enumerate(mates):
                copy = remote(times, times_all.at[q], t_send.at[m], t_recv.at[q], at(z, xx, cc))
                copy.start()
                sends.append(copy)
        after(i)
    for i in range(count - LAG_CORE, count):
        core_stage(i)
    for i in range(count - LAG_X, count):
        x_stage(i)
        if i == count - LAG_X + 1:
            for j in range(per - 1):
                finish(j)
    finish(per - 1)

    for j in range(per):
        for zz in others:
            there = gathered.at[zz * per + j]
            remote(there, there, a_send.at[0, j], a_recv.at[zz, j], at(zz, x, c)).wait_recv()

    for m, (xx, cc) in enumerate(mates):
        other = 2 * cc + xx
        remote(times, times_all.at[other], t_send.at[m], t_recv.at[other], at(z, xx, cc)).wait_recv()
        for w in range(2):
            picked[m, w] = gathered[times_all[other, 0, w]]
        copy = remote(picked.at[m], landed.at[q], p_send.at[m], p_recv.at[q], at(z, xx, cc))
        copy.start()
        sends.append(copy)
    for w in range(2):
        landed[q, w] = gathered[times[0, w]]
    for m, (xx, cc) in enumerate(mates):
        other = 2 * cc + xx
        remote(picked.at[m], landed.at[other], p_send.at[m], p_recv.at[other], at(z, xx, cc)).wait_recv()
    for copy in sends:
        copy.wait_send()


def pair_elementals(eigvecs, momentum, times, devices):
    slices, _, colors, width, sites = eigvecs.shape
    planes = devices // 4
    per = slices // planes
    half, quarter, both = width // 2, width // 4, 2 * width
    bf, f32 = jnp.bfloat16, jnp.float32
    dma = pltpu.SemaphoreType.DMA
    return pl.pallas_call(
        functools.partial(elemental_kernel, devices),
        out_shape=jax.ShapeDtypeStruct((4, 2, quarter, both), bf),
        in_specs=[
            pl.BlockSpec(memory_space=pltpu.HBM),
            pl.BlockSpec(memory_space=pltpu.HBM),
            pl.BlockSpec(memory_space=pltpu.HBM),
        ],
        out_specs=pl.BlockSpec(memory_space=pltpu.VMEM),
        scratch_shapes=[
            pltpu.VMEM((slices, 2, colors, width, sites), bf),
            pltpu.VMEM((slices, width, both), f32),
            pltpu.VMEM((slices, width, both), bf),
            pltpu.VMEM((slices, half, both), bf),
            pltpu.VMEM((slices, half, both), f32),
            pltpu.VMEM((slices, half, both), bf),
            pltpu.VMEM((slices, quarter, both), bf),
            pltpu.VMEM((slices, quarter, both), bf),
            pltpu.VMEM((planes, per, quarter, both), bf),
            pltpu.VMEM((slices, quarter, both), bf),
            pltpu.VMEM((3, 2, quarter, both), bf),
            pltpu.SMEM((4, 1, 2), jnp.int32),
            pltpu.SMEM(momentum.shape, jnp.int32),
            pltpu.SMEM(times.shape, jnp.int32),
            dma((2,)),
            dma((slices,)),
            dma((slices,)), dma((slices,)), dma((slices,)), dma((slices,)),
            dma((slices,)), dma((planes, per)),
            dma((planes, per)), dma((planes, per)),
            dma((3,)), dma((4,)),
            dma((3,)), dma((4,)),
        ],
        compiler_params=pltpu.CompilerParams(
            collective_id=0, has_side_effects=True, vmem_limit_bytes=25165824
        ),
    )(*(pltpu.with_memory_space_constraint(v, pltpu.HBM) for v in (momentum, times, eigvecs)))


def blocks_kernel(elementals, peram, out, staged, done):
    width = elementals.shape[3] // 2
    sink_el = jnp.concatenate([elementals[r, 0] for r in range(4)], axis=0)
    src_el = jnp.concatenate([elementals[r, 1] for r in range(4)], axis=0)
    a_re = sink_el[:, :width]
    a_im = sink_el[:, width:]
    upper = jnp.concatenate([a_re, -a_im], axis=1)
    lower = jnp.concatenate([a_im, a_re], axis=1)
    left = jnp.concatenate([upper, lower], axis=0)
    e_re = src_el[:, :width]
    e_im = src_el[:, width:]
    stores = []
    for a in range(4):
        rows = pl.ds((a + 2) % 4 * width, width)
        stacked = jnp.concatenate([peram[0, 0, rows], peram[0, 1, rows]], axis=0)
        x = jnp.dot(left, stacked, preferred_element_type=jnp.float32)
        x = (x if a < 2 else -x).astype(jnp.bfloat16)
        reals, imags = [], []
        for b in range(4):
            s = (b + 2) % 4
            piece = x[:, s * width:(s + 1) * width]
            by_re = lax.dot_general(piece, e_re, NT_DIMS, preferred_element_type=jnp.float32)
            by_im = lax.dot_general(piece, e_im, NT_DIMS, preferred_element_type=jnp.float32)
            reals.append(by_re[:width] + by_im[width:])
            imags.append(by_re[width:] - by_im[:width])
        here = pl.ds(a * width, width)
        staged[0, here] = jnp.concatenate(reals, axis=1).astype(jnp.bfloat16)
        staged[1, here] = jnp.concatenate(imags, axis=1).astype(jnp.bfloat16)
        store = pltpu.make_async_copy(staged.at[:, here], out.at[0, :, here], done.at[a])
        store.start()
        stores.append(store)
    for store in stores:
        store.wait()


def meson_blocks(elementals, peram):
    return pl.pallas_call(
        blocks_kernel,
        out_shape=jax.ShapeDtypeStruct(peram.shape, peram.dtype),
        in_specs=[pl.BlockSpec(memory_space=pltpu.VMEM), pl.BlockSpec(memory_space=pltpu.VMEM)],
        out_specs=pl.BlockSpec(memory_space=pltpu.HBM),
        scratch_shapes=[
            pltpu.VMEM(peram.shape[1:], peram.dtype),
            pltpu.SemaphoreType.DMA((4,)),
        ],
        compiler_params=pltpu.CompilerParams(vmem_limit_bytes=25165824),
    )(elementals, peram)


def summed_elementals(eigvecs, momentum, times, devices):
    device = lax.axis_index("sink")
    theta = angles(momentum, eigvecs.shape[-1], devices, device)
    cosine = jnp.cos(theta)
    sine = jnp.sin(theta)
    vec_re = eigvecs[:, 0]
    vec_im = eigvecs[:, 1]
    f_re = vec_re.astype(jnp.float32)
    f_im = vec_im.astype(jnp.float32)
    rot_re = (cosine * f_re + sine * f_im).astype(jnp.bfloat16)
    rot_im = (cosine * f_im - sine * f_re).astype(jnp.bfloat16)
    form = "tckx,tclx->tkl"
    dot = functools.partial(jnp.einsum, form, preferred_element_type=jnp.float32)
    real = dot(vec_re, rot_re) + dot(vec_im, rot_im)
    imag = dot(vec_re, rot_im) - dot(vec_im, rot_re)
    totals = lax.psum(jnp.concatenate([real, imag], axis=-1), "sink")
    picked = jnp.take(totals.astype(jnp.bfloat16), times[0], axis=0)
    quarter = picked.shape[1] // 4
    return picked.reshape(2, 4, quarter, picked.shape[2]).transpose(1, 0, 2, 3)


def shards(eigvecs, momentum, peram, times):
    devices = lax.axis_size("sink")
    if devices == 16 and eigvecs.shape[0] % 8 == 0:
        elementals = pair_elementals(eigvecs, momentum, times, devices)
    else:
        elementals = summed_elementals(eigvecs, momentum, times, devices)
    return meson_blocks(elementals, peram)


def solution(mesh):
    in_specs = (
        P("groups", None, None, None, "sink"),
        P("groups"),
        P(("groups", "sink"), None, None, None),
        P(("groups", "sink"), None),
    )
    out_specs = P(("groups", "sink"), None, None, None)
    return jax.shard_map(shards, mesh=mesh, in_specs=in_specs, out_specs=out_specs, check_vma=False)
```

```python
import functools
import math

import jax
import jax.numpy as jnp
from jax import lax
from jax.experimental import pallas as pl
from jax.experimental.pallas import tpu as pltpu
from jax.sharding import PartitionSpec as P

MESH = pl.DeviceIdType.MESH
NT_DIMS = (((1,), (1,)), ((), ()))
LAG_CORE = 1
LAG_X = 4
AHEAD = 4


def angles(momentum, sites, devices, device):
    local = jnp.arange(sites, dtype=jnp.int32)
    second = local // 16
    third = local % 16
    extent = sites // 16
    frac = jnp.mod(momentum[0] * device, devices).astype(jnp.float32) / devices
    frac = frac + jnp.mod(momentum[1] * second, extent).astype(jnp.float32) / extent
    frac = frac + jnp.mod(momentum[2] * third, 16).astype(jnp.float32) / 16.0
    return 2.0 * math.pi * frac


def wrap(value, size):
    if size & (size - 1) == 0:
        return value & (size - 1)
    return lax.rem(lax.rem(value, size) + size, size)


def elemental_kernel(devices, mom_hbm, times_hbm, eig, landed, tiles, own1, send1, got1, own2, send2, got2,
                     sendz, gotz, own3, sendf, gotf, gathered, picked, times_all, mom, times, small_sem,
                     load_sem, c_send, c_recv, x_send, x_recv, z_send, z_recv, f_send, f_recv,
                     a_send, a_recv, p_send, p_recv, t_send, t_recv):
    slices, _, colors, width, sites = eig.shape
    own = slices // 2
    half, quarter = width // 2, width // 4
    me = lax.axis_index("sink")
    x = lax.rem(lax.div(me, 2), 2)
    z = lax.div(me, 4)
    c = me & 1
    q = 2 * c + x

    def at(zz, xx, cc):
        return {"sink": (zz * 2 + xx) * 2 + cc}

    core_mate = at(z, x, 1 - c)
    x_mate = at(z, 1 - x, c)
    mates = [(1 - x, c), (x, 1 - c), (1 - x, 1 - c)]

    parity = lax.rem(z, 2)
    near = at(z + 1 - 2 * parity, x, c)
    far = at(lax.rem(z + 2, 4), x, c)
    mine = parity * own
    theirs = (1 - parity) * own

    steps = [theirs + k for k in range(own)] + [mine + k for k in range(own)]
    count = len(steps)

    mom_load = pltpu.make_async_copy(mom_hbm, mom, small_sem.at[0])
    mom_load.start()
    times_load = pltpu.make_async_copy(times_hbm, times, small_sem.at[1])
    times_load.start()
    loads = []
    for i, slot in enumerate(steps):
        load = pltpu.make_async_copy(eig.at[slot], tiles.at[i], load_sem.at[i])
        loads.append(load)
        if i < AHEAD:
            load.start()

    barrier = pltpu.get_barrier_semaphore()
    for xx, cc in mates:
        pl.semaphore_signal(barrier, inc=1, device_id=at(z, xx, cc), device_id_type=MESH)
    for other in (near, far):
        pl.semaphore_signal(barrier, inc=1, device_id=other, device_id_type=MESH)

    mom_load.wait()
    extent = sites // 16
    local = lax.broadcasted_iota(jnp.int32, (8, sites), 1)
    second = local >> 4
    third = local & 15
    first = wrap(mom[0] * me, devices).astype(jnp.float32) / devices
    frac = first + wrap(mom[1] * second, extent).astype(jnp.float32) / extent
    frac = frac + wrap(mom[2] * third, 16).astype(jnp.float32) / 16.0
    theta = (2.0 * math.pi) * frac
    cosine = jnp.cos(theta)[0:1]
    sine = jnp.sin(theta)[0:1]

    def remote(src, dst, ssem, rsem, dev):
        return pltpu.make_async_remote_copy(src_ref=src, dst_ref=dst, send_sem=ssem, recv_sem=rsem,
                                            device_id=dev, device_id_type=MESH)

    sends = []
    core_copies, x_copies = [], []

    def partial_sum(i):
        rot_re, rot_im, neg_re, vec_re, vec_im = [], [], [], [], []
        for col in range(colors):
            v_re = tiles[i, 0, col]
            v_im = tiles[i, 1, col]
            f_re = v_re.astype(jnp.float32)
            f_im = v_im.astype(jnp.float32)
            r_re = (cosine * f_re + sine * f_im).astype(jnp.bfloat16)
            rot_re.append(r_re)
            neg_re.append(-r_re)
            rot_im.append((cosine * f_im - sine * f_re).astype(jnp.bfloat16))
            vec_re.append(v_re)
            vec_im.append(v_im)
        both = jnp.concatenate(vec_re + vec_im, axis=1)
        for_re = jnp.concatenate(rot_re + rot_im, axis=1)
        for_im = jnp.concatenate(rot_im + neg_re, axis=1)
        real = lax.dot_general(both, for_re, NT_DIMS, preferred_element_type=jnp.float32)
        imag = lax.dot_general(both, for_im, NT_DIMS, preferred_element_type=jnp.float32)
        total = jnp.concatenate([real, imag], axis=1)
        own1[i] = total
        send1[i] = total.astype(jnp.bfloat16)

    def start_core(i):
        rows = pl.ds(pl.multiple_of((1 - c) * half, half), half)
        copy = remote(send1.at[i, rows], got1.at[i], c_send.at[i], c_recv.at[i], core_mate)
        copy.start()
        core_copies.append(copy)
        sends.append(copy)

    def core_stage(i):
        core_copies[i].wait_recv()
        total = own1[i, pl.ds(pl.multiple_of(c * half, half), half)] + got1[i].astype(jnp.float32)
        own2[i] = total
        send2[i] = total.astype(jnp.bfloat16)
        rows = pl.ds(pl.multiple_of((1 - x) * quarter, quarter), quarter)
        copy = remote(send2.at[i, rows], got2.at[i], x_send.at[i], x_recv.at[i], x_mate)
        copy.start()
        x_copies.append(copy)
        sends.append(copy)

    def from_near(k):
        return remote(sendz.at[k], gotz.at[k], z_send.at[k], z_recv.at[k], near)

    def from_far(k):
        return remote(sendf.at[k], gotf.at[k], f_send.at[k], f_recv.at[k], far)

    def x_stage(i):
        x_copies[i].wait_recv()
        total = own2[i, pl.ds(pl.multiple_of(x * quarter, quarter), quarter)] + got2[i].astype(jnp.float32)
        if i < own:
            sendz[i] = total.astype(jnp.bfloat16)
            copy = from_near(i)
        else:
            k = i - own
            from_near(k).wait_recv()
            total = total + gotz[k].astype(jnp.float32)
            own3[k] = total
            sendf[k] = total.astype(jnp.bfloat16)
            copy = from_far(k)
        copy.start()
        sends.append(copy)

    def finish(k):
        from_far(k).wait_recv()
        block = gathered.at[mine + k]
        gathered[mine + k] = (own3[k] + gotf[k].astype(jnp.float32)).astype(jnp.bfloat16)
        copy = remote(block, block, a_send.at[k], a_recv.at[k], near)
        copy.start()
        sends.append(copy)

    def after(i):
        start_core(i)
        if i >= LAG_CORE:
            core_stage(i - LAG_CORE)
        if i >= LAG_X:
            x_stage(i - LAG_X)

    for i in range(count):
        loads[i].wait()
        if i + AHEAD < count:
            loads[i + AHEAD].start()
        partial_sum(i)
        if i == 0:
            pl.semaphore_wait(barrier, len(mates) + 2)
            times_load.wait()
            for m, (xx, cc) in enumerate(mates):
                copy = remote(times, times_all.at[q], t_send.at[m], t_recv.at[q], at(z, xx, cc))
                copy.start()
                sends.append(copy)
        after(i)
    for i in range(count - LAG_CORE, count):
        core_stage(i)
    for i in range(count - LAG_X, count):
        x_stage(i)
    for k in range(own):
        finish(k)
    for k in range(own):
        there = gathered.at[theirs + k]
        remote(there, there, a_send.at[k], a_recv.at[k], near).wait_recv()

    for m, (xx, cc) in enumerate(mates):
        other = 2 * cc + xx
        remote(times, times_all.at[other], t_send.at[m], t_recv.at[other], at(z, xx, cc)).wait_recv()
        for w in range(2):
            picked[m, w] = gathered[times_all[other, 0, w]]
        copy = remote(picked.at[m], landed.at[q], p_send.at[m], p_recv.at[q], at(z, xx, cc))
        copy.start()
        sends.append(copy)
    for w in range(2):
        landed[q, w] = gathered[times[0, w]]
    for m, (xx, cc) in enumerate(mates):
        other = 2 * cc + xx
        remote(picked.at[m], landed.at[other], p_send.at[m], p_recv.at[other], at(z, xx, cc)).wait_recv()
    for copy in sends:
        copy.wait_send()


def pair_elementals(eigvecs, momentum, times, devices):
    slices, _, colors, width, sites = eigvecs.shape
    own = slices // 2
    half, quarter, both = width // 2, width // 4, 2 * width
    bf, f32 = jnp.bfloat16, jnp.float32
    dma = pltpu.SemaphoreType.DMA
    return pl.pallas_call(
        functools.partial(elemental_kernel, devices),
        out_shape=jax.ShapeDtypeStruct((4, 2, quarter, both), bf),
        in_specs=[
            pl.BlockSpec(memory_space=pltpu.HBM),
            pl.BlockSpec(memory_space=pltpu.HBM),
            pl.BlockSpec(memory_space=pltpu.HBM),
        ],
        out_specs=pl.BlockSpec(memory_space=pltpu.VMEM),
        scratch_shapes=[
            pltpu.VMEM((slices, 2, colors, width, sites), bf),
            pltpu.VMEM((slices, width, both), f32),
            pltpu.VMEM((slices, width, both), bf),
            pltpu.VMEM((slices, half, both), bf),
            pltpu.VMEM((slices, half, both), f32),
            pltpu.VMEM((slices, half, both), bf),
            pltpu.VMEM((slices, quarter, both), bf),
            pltpu.VMEM((own, quarter, both), bf),
            pltpu.VMEM((own, quarter, both), bf),
            pltpu.VMEM((own, quarter, both), f32),
            pltpu.VMEM((own, quarter, both), bf),
            pltpu.VMEM((own, quarter, both), bf),
            pltpu.VMEM((slices, quarter, both), bf),
            pltpu.VMEM((3, 2, quarter, both), bf),
            pltpu.SMEM((4, 1, 2), jnp.int32),
            pltpu.SMEM(momentum.shape, jnp.int32),
            pltpu.SMEM(times.shape, jnp.int32),
            dma((2,)),
            dma((slices,)),
            dma((slices,)), dma((slices,)), dma((slices,)), dma((slices,)),
            dma((own,)), dma((own,)), dma((own,)), dma((own,)),
            dma((own,)), dma((own,)),
            dma((3,)), dma((4,)),
            dma((3,)), dma((4,)),
        ],
        compiler_params=pltpu.CompilerParams(
            collective_id=0, has_side_effects=True, vmem_limit_bytes=25165824
        ),
    )(*(pltpu.with_memory_space_constraint(v, pltpu.HBM) for v in (momentum, times, eigvecs)))


def blocks_kernel(elementals, peram, out, staged, done):
    width = elementals.shape[3] // 2
    sink_el = jnp.concatenate([elementals[r, 0] for r in range(4)], axis=0)
    src_el = jnp.concatenate([elementals[r, 1] for r in range(4)], axis=0)
    a_re = sink_el[:, :width]
    a_im = sink_el[:, width:]
    upper = jnp.concatenate([a_re, -a_im], axis=1)
    lower = jnp.concatenate([a_im, a_re], axis=1)
    left = jnp.concatenate([upper, lower], axis=0)
    e_re = src_el[:, :width]
    e_im = src_el[:, width:]
    stores = []
    for a in range(4):
        rows = pl.ds((a + 2) % 4 * width, width)
        stacked = jnp.concatenate([peram[0, 0, rows], peram[0, 1, rows]], axis=0)
        x = jnp.dot(left, stacked, preferred_element_type=jnp.float32)
        x = (x if a < 2 else -x).astype(jnp.bfloat16)
        reals, imags = [], []
        for b in range(4):
            s = (b + 2) % 4
            piece = x[:, s * width:(s + 1) * width]
            by_re = lax.dot_general(piece, e_re, NT_DIMS, preferred_element_type=jnp.float32)
            by_im = lax.dot_general(piece, e_im, NT_DIMS, preferred_element_type=jnp.float32)
            reals.append(by_re[:width] + by_im[width:])
            imags.append(by_re[width:] - by_im[:width])
        here = pl.ds(a * width, width)
        staged[0, here] = jnp.concatenate(reals, axis=1).astype(jnp.bfloat16)
        staged[1, here] = jnp.concatenate(imags, axis=1).astype(jnp.bfloat16)
        store = pltpu.make_async_copy(staged.at[:, here], out.at[0, :, here], done.at[a])
        store.start()
        stores.append(store)
    for store in stores:
        store.wait()


def meson_blocks(elementals, peram):
    return pl.pallas_call(
        blocks_kernel,
        out_shape=jax.ShapeDtypeStruct(peram.shape, peram.dtype),
        in_specs=[pl.BlockSpec(memory_space=pltpu.VMEM), pl.BlockSpec(memory_space=pltpu.VMEM)],
        out_specs=pl.BlockSpec(memory_space=pltpu.HBM),
        scratch_shapes=[
            pltpu.VMEM(peram.shape[1:], peram.dtype),
            pltpu.SemaphoreType.DMA((4,)),
        ],
        compiler_params=pltpu.CompilerParams(vmem_limit_bytes=25165824),
    )(elementals, peram)


def summed_elementals(eigvecs, momentum, times, devices):
    device = lax.axis_index("sink")
    theta = angles(momentum, eigvecs.shape[-1], devices, device)
    cosine = jnp.cos(theta)
    sine = jnp.sin(theta)
    vec_re = eigvecs[:, 0]
    vec_im = eigvecs[:, 1]
    f_re = vec_re.astype(jnp.float32)
    f_im = vec_im.astype(jnp.float32)
    rot_re = (cosine * f_re + sine * f_im).astype(jnp.bfloat16)
    rot_im = (cosine * f_im - sine * f_re).astype(jnp.bfloat16)
    form = "tckx,tclx->tkl"
    dot = functools.partial(jnp.einsum, form, preferred_element_type=jnp.float32)
    real = dot(vec_re, rot_re) + dot(vec_im, rot_im)
    imag = dot(vec_re, rot_im) - dot(vec_im, rot_re)
    totals = lax.psum(jnp.concatenate([real, imag], axis=-1), "sink")
    picked = jnp.take(totals.astype(jnp.bfloat16), times[0], axis=0)
    quarter = picked.shape[1] // 4
    return picked.reshape(2, 4, quarter, picked.shape[2]).transpose(1, 0, 2, 3)


def shards(eigvecs, momentum, peram, times):
    devices = lax.axis_size("sink")
    if devices == 16 and eigvecs.shape[0] % 8 == 0:
        elementals = pair_elementals(eigvecs, momentum, times, devices)
    else:
        elementals = summed_elementals(eigvecs, momentum, times, devices)
    return meson_blocks(elementals, peram)


def solution(mesh):
    in_specs = (
        P("groups", None, None, None, "sink"),
        P("groups"),
        P(("groups", "sink"), None, None, None),
        P(("groups", "sink"), None),
    )
    out_specs = P(("groups", "sink"), None, None, None)
    return jax.shard_map(shards, mesh=mesh, in_specs=in_specs, out_specs=out_specs, check_vma=False)
```
